32 devices in a mesh: trow: 8 (over y, x, core), tcol: 4 (over z).
Axes of the slice: x: 2, y: 2, z: 4, core: 2. Of those that a mesh axis runs over, the one named last changes fastest.
Arguments:
- theta: float32 [25, 128, 1024], P(None, 'trow', 'tcol'), may hold values from -6 to 6
- salt: float32 [25, 128, 1024], P(None, 'trow', 'tcol'), may hold values from -6 to 6
- velocity_x: float32 [25, 128, 1024], P(None, 'trow', 'tcol'), may hold values from -0.5 to 0.5
- velocity_y: float32 [25, 128, 1024], P(None, 'trow', 'tcol'), may hold values from -0.5 to 0.5
- land_mask: int32 [25, 128, 1024], P(None, 'trow', 'tcol'), may hold values 0 or 1
- kappa: float32 [24, 128, 1024], P(None, 'trow', 'tcol'), may hold values from 0.02 to 5
- forcing: float32 [128, 1024], P('trow', 'tcol'), may hold values from -6 to 6
- bottom: int32 [128, 1024], P('trow', 'tcol'), may hold values from 0 to 25
- theta_cot: float32 [25, 128, 1024], P(None, 'trow', 'tcol'), may hold values from -6 to 6
- salt_cot: float32 [25, 128, 1024], P(None, 'trow', 'tcol'), may hold values from -6 to 6
- surface_cot: float32 [128, 1024], P('trow', 'tcol'), may hold values from -24 to 24
Outputs:
- theta_grad: float32 [25, 128, 1024], P(None, 'trow', 'tcol')
- salt_grad: float32 [25, 128, 1024], P(None, 'trow', 'tcol')
- kappa_grad: float32 [24, 128, 1024], P(None, 'trow', 'tcol')
- forcing_grad: float32 [128, 1024], P('trow', 'tcol')
The draws below stay inside these ranges and needn't reach their ends.
All inputs are finite; a program needn't handle non-finite values. No bound on the sum of `land_mask` on one device may be relied on, other than what follows from the above.
Results may differ from the reference program's by a relative error of at most 0.0001.
Values sent between devices are 32-bit elements; how exact they have to be, the bound alone decides.
A program may use at most 64 MiB of HBM per device.

```python
import math
import jax
import jax.numpy as jnp
from jax import lax

NZ = 25
KZ = 24
ITERS = 4
NX = 128
NY = 1024


def draw_surface_cot(key, part):
    row_position = jnp.arange(NX, dtype=jnp.float32) / NX
    col_position = jnp.arange(NY, dtype=jnp.float32) / NY
    rising = (3.0 ** row_position)[:, None] * (3.0 ** col_position)[None, :] / 3.0
    key_first = jax.random.fold_in(key, 0)
    values = jax.random.normal(key_first, (NX, NY), jnp.float32) * rising
    return jnp.clip(values, -24.0, 24.0)


def place_ends(result, stream_key, smallest, top_value):
    spot = [jax.random.randint(jax.random.fold_in(stream_key, axis), (), 0, length) for axis, length in enumerate(result.shape)]
    main_axis = result.shape.index(max(result.shape))
    next_to = spot[:main_axis] + [(spot[main_axis] + 1) % result.shape[main_axis]] + spot[main_axis + 1:]
    return result.at[tuple(spot)].set(smallest).at[tuple(next_to)].set(top_value)


def level_of(rng, extent, cuts, least, top_value):
    loudness = 1.0
    for position, parts in cuts:
        steps = jax.random.uniform(jax.random.fold_in(jax.random.fold_in(rng, 6), position), (parts,), jnp.float32, least / len(cuts), top_value / len(cuts))
        loudness = loudness * jnp.repeat(jnp.exp(steps), extent[position] // parts).reshape((-1,) + (1,) * (len(extent) - 1 - position))
    return loudness


def scatter_about(key, extent, scale, bound, cuts=(), kind=jnp.bfloat16):
    gain = level_of(key, extent, cuts, -0.22, 0.18) if cuts else 1.0
    drawn = jax.random.normal(key, extent, jnp.float32) * scale * gain
    return jnp.minimum(jnp.maximum(drawn, -bound), bound).astype(kind)


def setup_inputs(seed: int = 0) -> dict:
    streams_of = jax.random.split(jax.random.key(seed), 12)
    theta = scatter_about(streams_of[0], (NZ, NX, NY), 1.0, 6.0, ((1, 8), (2, 4)), jnp.float32)
    salt = scatter_about(streams_of[1], (NZ, NX, NY), 1.0, 6.0, ((1, 8), (2, 4)), jnp.float32)
    velocity_x = jnp.clip(jax.random.uniform(streams_of[2], (NZ, NX, NY), jnp.float32, -0.5, 0.5) * level_of(streams_of[2], (NZ, NX, NY), ((1, 8), (2, 4)), -0.4, 0.0), -0.5, 0.5)
    velocity_y = jnp.clip(jax.random.uniform(streams_of[3], (NZ, NX, NY), jnp.float32, -0.5, 0.5) * level_of(streams_of[3], (NZ, NX, NY), ((1, 8), (2, 4)), -0.4, 0.0), -0.5, 0.5)
    land_mask = place_ends((jax.random.randint(streams_of[4], (NZ, NX, NY), 0, 8) < 7).astype(jnp.int32), jax.random.fold_in(streams_of[4], 1), 0, 1)
    kappa = jnp.clip(jnp.exp(math.log(5.0) - 5.521461 * jax.random.uniform(streams_of[5], (KZ, NX, NY), jnp.float32) ** level_of(streams_of[5], (KZ, NX, NY), ((1, 8), (2, 4)), -0.2, 0.2)), 0.02, 5.0)
    forcing = scatter_about(streams_of[6], (NX, NY), 1.0, 6.0, ((0, 8), (1, 4)), jnp.float32)
    bottom = place_ends(jax.random.randint(streams_of[7], (NX, NY), 0, NZ + 1), jax.random.fold_in(streams_of[7], 1), 0, NZ).astype(jnp.int32)
    theta_cot = scatter_about(streams_of[8], (NZ, NX, NY), 1.0, 6.0, ((1, 8), (2, 4)), jnp.float32)
    salt_cot = scatter_about(streams_of[9], (NZ, NX, NY), 1.0, 6.0, ((1, 8), (2, 4)), jnp.float32)
    surface_cot = draw_surface_cot(jax.random.fold_in(streams_of[11], 71), 0)
    return {"theta": theta, "salt": salt, "velocity_x": velocity_x, "velocity_y": velocity_y, "land_mask": land_mask, "kappa": kappa, "forcing": forcing, "bottom": bottom, "theta_cot": theta_cot, "salt_cot": salt_cot, "surface_cot": surface_cot}


def cut_along(array, start, count, axis_index):
    return lax.slice_in_dim(array, start, start + count, axis=axis_index)


def forward_change(padded_tracer, padded_velocity, padded_wet, axis_index, length):
    opened = cut_along(padded_velocity, 1, length + 1, axis_index) * cut_along(padded_wet, 1, length + 1, axis_index) * cut_along(padded_wet, 2, length + 1, axis_index)
    centre = cut_along(padded_tracer, 1, length + 1, axis_index) + cut_along(padded_tracer, 2, length + 1, axis_index)
    outer = cut_along(padded_tracer, 0, length + 1, axis_index) + cut_along(padded_tracer, 3, length + 1, axis_index)
    fluxes = opened * (7.0 * centre - outer) / 12.0
    return cut_along(fluxes, 1, length, axis_index) - cut_along(fluxes, 0, length, axis_index)


def adjoint_change(padded_lambda, padded_velocity, padded_wet, axis_index, length):
    opened = cut_along(padded_velocity, 0, length + 3, axis_index) * cut_along(padded_wet, 0, length + 3, axis_index) * cut_along(padded_wet, 1, length + 3, axis_index)
    faces = opened * (cut_along(padded_lambda, 0, length + 3, axis_index) - cut_along(padded_lambda, 1, length + 3, axis_index))
    return (7.0 * (cut_along(faces, 2, length, axis_index) + cut_along(faces, 1, length, axis_index)) - cut_along(faces, 3, length, axis_index) - cut_along(faces, 0, length, axis_index)) / 12.0


def advect(padded_tracer, padded_ux, padded_uy, padded_wet, tracer):
    row_count = padded_tracer.shape[1] - 4
    col_count = padded_tracer.shape[2] - 4
    along_rows = forward_change(padded_tracer[:, :, 2:-2], padded_ux[:, :, 2:-2], padded_wet[:, :, 2:-2], 1, row_count)
    along_cols = forward_change(padded_tracer[:, 2:-2, :], padded_uy[:, 2:-2, :], padded_wet[:, 2:-2, :], 2, col_count)
    return tracer - along_rows - along_cols


def advect_adjoint(padded_lambda, padded_ux, padded_uy, padded_wet, lambda_field, wet):
    row_count = padded_lambda.shape[1] - 4
    col_count = padded_lambda.shape[2] - 4
    along_rows = adjoint_change(padded_lambda[:, :, 2:-2], padded_ux[:, :, 2:-2], padded_wet[:, :, 2:-2], 1, row_count)
    along_cols = adjoint_change(padded_lambda[:, 2:-2, :], padded_uy[:, 2:-2, :], padded_wet[:, 2:-2, :], 2, col_count)
    return lambda_field - wet * (along_rows + along_cols)


def factorize(couple, depth):
    inverses = []
    ratios = []
    for depth_index in range(depth):
        diagonal = jnp.ones_like(couple[0])
        if depth_index > 0:
            diagonal = diagonal + couple[depth_index - 1] - couple[depth_index - 1] * ratios[depth_index - 1]
        if depth_index < depth - 1:
            diagonal = diagonal + couple[depth_index]
        inverse = 1.0 / diagonal
        inverses.append(inverse)
        if depth_index < depth - 1:
            ratios.append(couple[depth_index] * inverse)
    return inverses, ratios


def solve_columns(inverses, ratios, couple, rhs):
    depth = rhs.shape[0]
    sweeps = []
    carried = rhs[0] * inverses[0]
    sweeps.append(carried)
    for depth_index in range(1, depth):
        carried = (rhs[depth_index] + couple[depth_index - 1] * carried) * inverses[depth_index]
        sweeps.append(carried)
    results = [sweeps[depth - 1]]
    for depth_index in range(depth - 2, -1, -1):
        results.append(sweeps[depth_index] + ratios[depth_index] * results[-1])
    return jnp.stack(results[::-1])


def pad_rims(array):
    return jnp.pad(array, ((0, 0), (2, 2), (2, 2)))


def surface_apply(field, diagonal):
    padded = jnp.pad(field, 1)
    beside = padded[2:, 1:-1] + padded[:-2, 1:-1] + padded[1:-1, 2:] + padded[1:-1, :-2]
    return diagonal * field - beside


def conjugate(target, diagonal):
    solution = jnp.zeros_like(target)
    residual = target
    direction = target
    norm_now = jnp.sum(residual * residual)
    for iteration in range(ITERS):
        image = surface_apply(direction, diagonal)
        step_size = norm_now / jnp.sum(direction * image)
        solution = solution + step_size * direction
        residual = residual - step_size * image
        if iteration + 1 < ITERS:
            norm_next = jnp.sum(residual * residual)
            direction = residual + (norm_next / norm_now) * direction
            norm_now = norm_next
    return solution


def reference(theta, salt, velocity_x, velocity_y, land_mask, kappa, forcing, bottom, theta_cot, salt_cot, surface_cot):
    depth = theta.shape[0]
    levels = jnp.arange(depth, dtype=jnp.int32)[:, None, None]
    wet = land_mask.astype(jnp.float32) * (levels < bottom[None]).astype(jnp.float32)
    padded_ux = pad_rims(velocity_x)
    padded_uy = pad_rims(velocity_y)
    padded_wet = pad_rims(wet)
    theta_adv = advect(pad_rims(theta * wet), padded_ux, padded_uy, padded_wet, theta)
    salt_adv = advect(pad_rims(salt * wet), padded_ux, padded_uy, padded_wet, salt)
    couple = [kappa[depth_index] * wet[depth_index] * wet[depth_index + 1] for depth_index in range(depth - 1)]
    inverses, ratios = factorize(couple, depth)
    source = jnp.concatenate([theta_adv[:1] + (forcing * wet[0])[None], theta_adv[1:]], axis=0)
    theta_mix = solve_columns(inverses, ratios, couple, source)
    salt_mix = solve_columns(inverses, ratios, couple, salt_adv)
    diagonal = 4.2 + bottom.astype(jnp.float32) / depth
    zeta = conjugate(surface_cot, diagonal)
    theta_total = theta_cot + 0.2 * wet * zeta[None]
    salt_total = salt_cot - 0.15 * wet * zeta[None]
    theta_mu = solve_columns(inverses, ratios, couple, theta_total)
    salt_mu = solve_columns(inverses, ratios, couple, salt_total)
    opened = wet[:-1] * wet[1:]
    kappa_grad = -opened * ((theta_mu[:-1] - theta_mu[1:]) * (theta_mix[:-1] - theta_mix[1:]) + (salt_mu[:-1] - salt_mu[1:]) * (salt_mix[:-1] - salt_mix[1:]))
    forcing_grad = zeta + wet[0] * theta_mu[0]
    theta_grad = advect_adjoint(pad_rims(theta_mu), padded_ux, padded_uy, padded_wet, theta_mu, wet)
    salt_grad = advect_adjoint(pad_rims(salt_mu), padded_ux, padded_uy, padded_wet, salt_mu, wet)
    return theta_grad, salt_grad, kappa_grad, forcing_grad
```

```python
import jax
import jax.numpy as jnp
from jax import lax
from jax.sharding import PartitionSpec as P

ITERS = 4


def padded_2(array, sides, width):
    for axis, dim in sides:
        peers, length = (lax.axis_size(axis), array.shape[dim])
        up = [(i, (i + 1) % peers) for i in range(peers - 1)]
        down = [(j, i) for i, j in up]
        last = lax.slice_in_dim(array, length - width, length, axis=dim)
        leading = lax.slice_in_dim(array, 0, width, axis=dim)
        before = lax.ppermute(last, axis, up)
        after = lax.ppermute(leading, axis, down)
        array = jnp.concatenate([before, array, after], axis=dim)
    return array


def cut_along(array, start, count, axis_index):
    return lax.slice_in_dim(array, start, start + count, axis=axis_index)


def forward_change(padded_tracer, padded_velocity, padded_wet, axis_index, length):
    opened = (
        cut_along(padded_velocity, 1, length + 1, axis_index)
        * cut_along(padded_wet, 1, length + 1, axis_index)
        * cut_along(padded_wet, 2, length + 1, axis_index)
    )
    centre = cut_along(padded_tracer, 1, length + 1, axis_index) + cut_along(
        padded_tracer, 2, length + 1, axis_index
    )
    outer = cut_along(padded_tracer, 0, length + 1, axis_index) + cut_along(
        padded_tracer, 3, length + 1, axis_index
    )
    fluxes = opened * (7.0 * centre - outer) / 12.0
    return cut_along(fluxes, 1, length, axis_index) - cut_along(fluxes, 0, length, axis_index)


def adjoint_change(padded_lambda, padded_velocity, padded_wet, axis_index, length):
    opened = (
        cut_along(padded_velocity, 0, length + 3, axis_index)
        * cut_along(padded_wet, 0, length + 3, axis_index)
        * cut_along(padded_wet, 1, length + 3, axis_index)
    )
    faces = opened * (
        cut_along(padded_lambda, 0, length + 3, axis_index)
        - cut_along(padded_lambda, 1, length + 3, axis_index)
    )
    return (
        7.0 * (cut_along(faces, 2, length, axis_index) + cut_along(faces, 1, length, axis_index))
        - cut_along(faces, 3, length, axis_index)
        - cut_along(faces, 0, length, axis_index)
    ) / 12.0


def advect(padded_tracer, padded_ux, padded_uy, padded_wet, tracer):
    row_count = padded_tracer.shape[1] - 4
    col_count = padded_tracer.shape[2] - 4
    along_rows = forward_change(
        padded_tracer[:, :, 2:-2], padded_ux[:, :, 2:-2], padded_wet[:, :, 2:-2], 1, row_count
    )
    along_cols = forward_change(
        padded_tracer[:, 2:-2, :], padded_uy[:, 2:-2, :], padded_wet[:, 2:-2, :], 2, col_count
    )
    return tracer - along_rows - along_cols


def advect_adjoint(padded_lambda, padded_ux, padded_uy, padded_wet, lambda_field, wet):
    row_count = padded_lambda.shape[1] - 4
    col_count = padded_lambda.shape[2] - 4
    along_rows = adjoint_change(
        padded_lambda[:, :, 2:-2], padded_ux[:, :, 2:-2], padded_wet[:, :, 2:-2], 1, row_count
    )
    along_cols = adjoint_change(
        padded_lambda[:, 2:-2, :], padded_uy[:, 2:-2, :], padded_wet[:, 2:-2, :], 2, col_count
    )
    return lambda_field - wet * (along_rows + along_cols)


def factorize(couple, depth):
    inverses = []
    ratios = []
    for depth_index in range(depth):
        diagonal = jnp.ones_like(couple[0])
        if depth_index > 0:
            diagonal = (
                diagonal
                + couple[depth_index - 1]
                - couple[depth_index - 1] * ratios[depth_index - 1]
            )
        if depth_index < depth - 1:
            diagonal = diagonal + couple[depth_index]
        inverse = 1.0 / diagonal
        inverses.append(inverse)
        if depth_index < depth - 1:
            ratios.append(couple[depth_index] * inverse)
    return (inverses, ratios)


def solve_columns(inverses, ratios, couple, rhs):
    depth = rhs.shape[0]
    sweeps = []
    carried = rhs[0] * inverses[0]
    sweeps.append(carried)
    for depth_index in range(1, depth):
        carried = (rhs[depth_index] + couple[depth_index - 1] * carried) * inverses[depth_index]
        sweeps.append(carried)
    results = [sweeps[depth - 1]]
    for depth_index in range(depth - 2, -1, -1):
        results.append(sweeps[depth_index] + ratios[depth_index] * results[-1])
    return jnp.stack(results[::-1])


LOW, HIGH = 0.2, 9.2
CENTRE, RADIUS = (HIGH + LOW) / 2, (HIGH - LOW) / 2


def times_operator(poly):
    out = [0.0] * (len(poly) + 1)
    for k, c in enumerate(poly):
        out[k] = out[k] + CENTRE * c
        if k == 0:
            out[1] = out[1] + RADIUS * c
        else:
            out[k + 1] = out[k + 1] + 0.5 * RADIUS * c
            out[k - 1] = out[k - 1] + 0.5 * RADIUS * c
    return out


def inner(p, q, moments):
    total = 0.0
    for i, a in enumerate(p):
        for j, b in enumerate(q):
            total = total + a * b * (0.5 * (moments[i + j] + moments[abs(i - j)]))
    return total


def add_scaled(p, scale, q):
    size = max(len(p), len(q))
    p = p + [0.0] * (size - len(p))
    q = q + [0.0] * (size - len(q))
    return [a + scale * b for a, b in zip(p, q)]


def weights_from(moments):
    residual = [jnp.ones_like(moments[0])]
    direction = residual
    result = []
    norm_now = moments[0]
    for iteration in range(ITERS):
        image = times_operator(direction)
        step = norm_now / inner(direction, image, moments)
        result = add_scaled(result, step, direction)
        if iteration + 1 < ITERS:
            residual = add_scaled(residual, -step, image)
            norm_next = inner(residual, residual, moments)
            direction = add_scaled(residual, norm_next / norm_now, direction)
            norm_now = norm_next
    return result


def conjugate(target, bottom, depth):
    rows, cols = target.shape
    rim = ITERS
    padded = padded_2(jnp.stack([target, bottom.astype(jnp.float32)]), (("trow", 1), ("tcol", 2)), rim)
    row = lax.broadcasted_iota(jnp.int32, (rows + 2 * rim, 1), 0) - rim + lax.axis_index("trow") * rows
    col = lax.broadcasted_iota(jnp.int32, (1, cols + 2 * rim), 1) - rim + lax.axis_index("tcol") * cols
    inside = ((row >= 0) & (row < rows * lax.axis_size("trow"))) & (
        (col >= 0) & (col < cols * lax.axis_size("tcol"))
    )
    scaled = (4.2 - CENTRE + padded[1] / depth) / RADIUS
    basis = [padded[0]]
    for k in range(ITERS):
        field = basis[-1]
        edge = k + 1
        beside = field[2:, 1:-1] + field[:-2, 1:-1] + field[1:-1, 2:] + field[1:-1, :-2]
        image = scaled[edge:-edge, edge:-edge] * field[1:-1, 1:-1] - beside * (1.0 / RADIUS)
        if k > 0:
            image = 2.0 * image - basis[-2][2:-2, 2:-2]
        basis.append(jnp.where(inside[edge:-edge, edge:-edge], image, 0.0))
    own = [f[rim - k : rim - k + rows, rim - k : rim - k + cols] for k, f in enumerate(basis)]
    sums = [jnp.sum(own[0] * own[k]) for k in range(5)]
    sums += [jnp.sum(own[2] * own[3]), jnp.sum(own[3] * own[3]), jnp.sum(own[3] * own[4])]
    m = list(lax.psum(jnp.stack(sums), ("trow", "tcol")))
    m = m[:5] + [2.0 * m[5] - m[1], 2.0 * m[6] - m[0], 2.0 * m[7] - m[1]]
    weights = weights_from(m)
    result = weights[0] * own[0]
    for k in range(1, ITERS):
        result = result + weights[k] * own[k]
    return result


def forward_state(padded, theta, salt, forcing, wet, inverses, ratios, couple):
    theta_adv = advect(padded[0], padded[2], padded[3], padded[4], theta)
    salt_adv = advect(padded[1], padded[2], padded[3], padded[4], salt)
    source = jnp.concatenate([theta_adv[:1] + (forcing * wet[0])[None], theta_adv[1:]], axis=0)
    theta_mix = solve_columns(inverses, ratios, couple, source)
    salt_mix = solve_columns(inverses, ratios, couple, salt_adv)
    return (theta_mix, salt_mix)


def mixing_adjoint(zeta, wet, theta_cot, salt_cot, inverses, ratios, couple):
    theta_total = theta_cot + 0.2 * wet * zeta[None]
    salt_total = salt_cot - 0.15 * wet * zeta[None]
    theta_mu = solve_columns(inverses, ratios, couple, theta_total)
    salt_mu = solve_columns(inverses, ratios, couple, salt_total)
    return (theta_mu, salt_mu)


def shards(
    theta,
    salt,
    velocity_x,
    velocity_y,
    land_mask,
    kappa,
    forcing,
    bottom,
    theta_cot,
    salt_cot,
    surface_cot,
):
    depth = theta.shape[0]
    levels = lax.broadcasted_iota(jnp.int32, (depth, 1, 1), 0)
    wet = land_mask.astype(jnp.float32) * (levels < bottom[None]).astype(jnp.float32)
    couple = [
        kappa[depth_index] * wet[depth_index] * wet[depth_index + 1]
        for depth_index in range(depth - 1)
    ]
    inverses, ratios = factorize(couple, depth)
    stacked = jnp.stack([theta * wet, salt * wet, velocity_x, velocity_y, wet])
    padded = padded_2(stacked, (("trow", 2), ("tcol", 3)), 2)
    theta_mix, salt_mix = forward_state(padded, theta, salt, forcing, wet, inverses, ratios, couple)
    zeta = conjugate(surface_cot, bottom, depth)
    theta_mu, salt_mu = mixing_adjoint(zeta, wet, theta_cot, salt_cot, inverses, ratios, couple)
    lambdas = padded_2(jnp.stack([theta_mu, salt_mu]), (("trow", 2), ("tcol", 3)), 2)
    padded_theta_mu = lambdas[0]
    padded_salt_mu = lambdas[1]
    opened = wet[:-1] * wet[1:]
    kappa_grad = -opened * (
        (theta_mu[:-1] - theta_mu[1:]) * (theta_mix[:-1] - theta_mix[1:])
        + (salt_mu[:-1] - salt_mu[1:]) * (salt_mix[:-1] - salt_mix[1:])
    )
    forcing_grad = zeta + wet[0] * theta_mu[0]
    theta_grad = advect_adjoint(padded_theta_mu, padded[2], padded[3], padded[4], theta_mu, wet)
    salt_grad = advect_adjoint(padded_salt_mu, padded[2], padded[3], padded[4], salt_mu, wet)
    return (theta_grad, salt_grad, kappa_grad, forcing_grad)


def solution(mesh):
    in_specs = (
        P(None, "trow", "tcol"),
        P(None, "trow", "tcol"),
        P(None, "trow", "tcol"),
        P(None, "trow", "tcol"),
        P(None, "trow", "tcol"),
        P(None, "trow", "tcol"),
        P("trow", "tcol"),
        P("trow", "tcol"),
        P(None, "trow", "tcol"),
        P(None, "trow", "tcol"),
        P("trow", "tcol"),
    )
    out_specs = (
        P(None, "trow", "tcol"),
        P(None, "trow", "tcol"),
        P(None, "trow", "tcol"),
        P("trow", "tcol"),
    )
    return jax.shard_map(shards, mesh=mesh, in_specs=in_specs, out_specs=out_specs, check_vma=False)
```

```python
import jax
import jax.numpy as jnp
from jax import lax
from jax.experimental import pallas as pl
from jax.experimental.pallas import tpu as pltpu
from jax.sharding import PartitionSpec as P

ITERS = 4


def padded_2(array, sides, width):
    for axis, dim in sides:
        peers, length = (lax.axis_size(axis), array.shape[dim])
        up = [(i, (i + 1) % peers) for i in range(peers - 1)]
        down = [(j, i) for i, j in up]
        last = lax.slice_in_dim(array, length - width, length, axis=dim)
        leading = lax.slice_in_dim(array, 0, width, axis=dim)
        before = lax.ppermute(last, axis, up)
        after = lax.ppermute(leading, axis, down)
        array = jnp.concatenate([before, array, after], axis=dim)
    return array


def cut_along(array, start, count, axis_index):
    return lax.slice_in_dim(array, start, start + count, axis=axis_index)


def join(before, array, after, axis):
    return jnp.concatenate([before, array, after], axis=axis)


def open_faces(velocity, wet, first, count, axis):
    return (
        cut_along(velocity, first, count, axis)
        * cut_along(wet, first, count, axis)
        * cut_along(wet, first + 1, count, axis)
    )


def forward_change(tracer, opened, axis, length):
    centre = cut_along(tracer, 1, length + 1, axis) + cut_along(tracer, 2, length + 1, axis)
    outer = cut_along(tracer, 0, length + 1, axis) + cut_along(tracer, 3, length + 1, axis)
    fluxes = opened * (7.0 * centre - outer) * (1.0 / 12.0)
    return cut_along(fluxes, 1, length, axis) - cut_along(fluxes, 0, length, axis)


def adjoint_change(field, opened, axis, length):
    faces = opened * (cut_along(field, 0, length + 3, axis) - cut_along(field, 1, length + 3, axis))
    return (
        7.0 * (cut_along(faces, 2, length, axis) + cut_along(faces, 1, length, axis))
        - cut_along(faces, 3, length, axis)
        - cut_along(faces, 0, length, axis)
    ) * (1.0 / 12.0)


def wet_at(land, bottom, k):
    return jnp.where(k < bottom[...], land[k].astype(jnp.float32), 0.0)


def couple_at(kappa, land, bottom, k, depth):
    below = jnp.minimum(k + 1, depth - 1)
    value = kappa[jnp.minimum(k, depth - 2)] * wet_at(land, bottom, k) * wet_at(land, bottom, below)
    return jnp.where(k < depth - 1, value, 0.0)


def rows_of(rb, ra, index, k, own):
    return join(rb[index, k], own, ra[index, k], 0)


def cols_of(rim, index, k, own):
    edge = rim[index, k]
    return join(edge[:, :2], own, edge[:, 2:], 1)


def forward_kernel(
    theta, salt, vx, vy, land, kappa, forcing, bottom, rb, ra, rim, theta_mix, salt_mix, ratios
):
    depth, rows, cols = theta.shape

    def down(k, carry):
        couple_before, ratio_before, theta_before, salt_before = carry
        wet = wet_at(land, bottom, k)
        couple = couple_at(kappa, land, bottom, k, depth)
        inverse = 1.0 / (1.0 + couple_before - couple_before * ratio_before + couple)
        ratio = couple * inverse
        ratios[k] = ratio
        open_x = open_faces(
            rows_of(rb, ra, 2, k, vx[k]), rows_of(rb, ra, 3, k, wet), 1, rows + 1, 0
        )
        open_y = open_faces(cols_of(rim, 2, k, vy[k]), cols_of(rim, 3, k, wet), 1, cols + 1, 1)
        found = []
        for index, (tracer, before) in enumerate(((theta, theta_before), (salt, salt_before))):
            own = tracer[k]
            masked = own * wet
            adv = (
                own
                - forward_change(rows_of(rb, ra, index, k, masked), open_x, 0, rows)
                - forward_change(cols_of(rim, index, k, masked), open_y, 1, cols)
            )
            if index == 0:
                adv = adv + jnp.where(k == 0, forcing[...] * wet, 0.0)
            found.append((adv + couple_before * before) * inverse)
        theta_mix[k] = found[0]
        salt_mix[k] = found[1]
        return couple, ratio, found[0], found[1]

    zero = jnp.zeros((rows, cols), jnp.float32)
    _, _, theta_last, salt_last = lax.fori_loop(0, depth, down, (zero, zero, zero, zero))

    def up(i, carry):
        k = depth - 2 - i
        a = theta_mix[k] + ratios[k] * carry[0]
        b = salt_mix[k] + ratios[k] * carry[1]
        theta_mix[k] = a
        salt_mix[k] = b
        return a, b

    lax.fori_loop(0, depth - 1, up, (theta_last, salt_last))


def mixing_kernel(
    theta_cot, salt_cot, land, kappa, bottom, zeta, theta_mix, salt_mix,
    theta_mu, salt_mu, kappa_grad, forcing_grad, ratios
):
    depth, rows, cols = theta_cot.shape

    def down(k, carry):
        couple_before, ratio_before, theta_before, salt_before = carry
        lifted = wet_at(land, bottom, k) * zeta[...]
        couple = couple_at(kappa, land, bottom, k, depth)
        inverse = 1.0 / (1.0 + couple_before - couple_before * ratio_before + couple)
        ratio = couple * inverse
        ratios[k] = ratio
        a = (theta_cot[k] + 0.2 * lifted + couple_before * theta_before) * inverse
        b = (salt_cot[k] - 0.15 * lifted + couple_before * salt_before) * inverse
        theta_mu[k] = a
        salt_mu[k] = b
        return couple, ratio, a, b

    zero = jnp.zeros((rows, cols), jnp.float32)
    _, _, theta_last, salt_last = lax.fori_loop(0, depth, down, (zero, zero, zero, zero))

    def up(i, carry):
        k = depth - 2 - i
        a = theta_mu[k] + ratios[k] * carry[0]
        b = salt_mu[k] + ratios[k] * carry[1]
        theta_mu[k] = a
        salt_mu[k] = b
        opened = wet_at(land, bottom, k) * wet_at(land, bottom, k + 1)
        kappa_grad[k] = -opened * (
            (a - carry[0]) * (theta_mix[k] - theta_mix[k + 1])
            + (b - carry[1]) * (salt_mix[k] - salt_mix[k + 1])
        )
        return a, b

    theta_top, _ = lax.fori_loop(0, depth - 1, up, (theta_last, salt_last))
    forcing_grad[...] = zeta[...] + wet_at(land, bottom, 0) * theta_top


def adjoint_kernel(
    theta_mu, salt_mu, vx, vy, land, bottom, rb, ra, rim, mu_rb, mu_ra, mu_rim, theta_grad, salt_grad
):
    depth, rows, cols = theta_mu.shape

    def level(k, carry):
        wet = wet_at(land, bottom, k)
        open_x = open_faces(
            rows_of(rb, ra, 2, k, vx[k]), rows_of(rb, ra, 3, k, wet), 0, rows + 3, 0
        )
        open_y = open_faces(cols_of(rim, 2, k, vy[k]), cols_of(rim, 3, k, wet), 0, cols + 3, 1)
        for index, (field, out) in enumerate(((theta_mu, theta_grad), (salt_mu, salt_grad))):
            own = field[k]
            out[k] = own - wet * (
                adjoint_change(rows_of(mu_rb, mu_ra, index, k, own), open_x, 0, rows)
                + adjoint_change(cols_of(mu_rim, index, k, own), open_y, 1, cols)
            )
        return carry

    lax.fori_loop(0, depth, level, 0)


LOW, HIGH = 0.2, 9.2
CENTRE, RADIUS = (HIGH + LOW) / 2, (HIGH - LOW) / 2


def times_operator(poly):
    out = [0.0] * (len(poly) + 1)
    for k, c in enumerate(poly):
        out[k] = out[k] + CENTRE * c
        if k == 0:
            out[1] = out[1] + RADIUS * c
        else:
            out[k + 1] = out[k + 1] + 0.5 * RADIUS * c
            out[k - 1] = out[k - 1] + 0.5 * RADIUS * c
    return out


def inner(p, q, moments):
    total = 0.0
    for i, a in enumerate(p):
        for j, b in enumerate(q):
            total = total + a * b * (0.5 * (moments[i + j] + moments[abs(i - j)]))
    return total


def add_scaled(p, scale, q):
    size = max(len(p), len(q))
    p = p + [0.0] * (size - len(p))
    q = q + [0.0] * (size - len(q))
    return [a + scale * b for a, b in zip(p, q)]


def weights_from(moments):
    residual = [jnp.ones_like(moments[0])]
    direction = residual
    result = []
    norm_now = moments[0]
    for iteration in range(ITERS):
        image = times_operator(direction)
        step = norm_now / inner(direction, image, moments)
        result = add_scaled(result, step, direction)
        if iteration + 1 < ITERS:
            residual = add_scaled(residual, -step, image)
            norm_next = inner(residual, residual, moments)
            direction = add_scaled(residual, norm_next / norm_now, direction)
            norm_now = norm_next
    return result


def conjugate(target, bottom, depth):
    rows, cols = target.shape
    rim = ITERS
    padded = padded_2(jnp.stack([target, bottom.astype(jnp.float32)]), (("trow", 1), ("tcol", 2)), rim)
    row = lax.broadcasted_iota(jnp.int32, (rows + 2 * rim, 1), 0) - rim + lax.axis_index("trow") * rows
    col = lax.broadcasted_iota(jnp.int32, (1, cols + 2 * rim), 1) - rim + lax.axis_index("tcol") * cols
    inside = ((row >= 0) & (row < rows * lax.axis_size("trow"))) & (
        (col >= 0) & (col < cols * lax.axis_size("tcol"))
    )
    scaled = (4.2 - CENTRE + padded[1] / depth) / RADIUS
    basis = [padded[0]]
    for k in range(ITERS):
        field = basis[-1]
        edge = k + 1
        beside = field[2:, 1:-1] + field[:-2, 1:-1] + field[1:-1, 2:] + field[1:-1, :-2]
        image = scaled[edge:-edge, edge:-edge] * field[1:-1, 1:-1] - beside * (1.0 / RADIUS)
        if k > 0:
            image = 2.0 * image - basis[-2][2:-2, 2:-2]
        basis.append(jnp.where(inside[edge:-edge, edge:-edge], image, 0.0))
    own = [f[rim - k : rim - k + rows, rim - k : rim - k + cols] for k, f in enumerate(basis)]
    sums = [jnp.sum(own[0] * own[k]) for k in range(5)]
    sums += [jnp.sum(own[2] * own[3]), jnp.sum(own[3] * own[3]), jnp.sum(own[3] * own[4])]
    m = list(lax.psum(jnp.stack(sums), ("trow", "tcol")))
    m = m[:5] + [2.0 * m[5] - m[1], 2.0 * m[6] - m[0], 2.0 * m[7] - m[1]]
    weights = weights_from(m)
    result = weights[0] * own[0]
    for k in range(1, ITERS):
        result = result + weights[k] * own[k]
    return result


def call(kernel, outs, scratch, args):
    size = sum(a.size for a in args) * 4
    return pl.pallas_call(
        kernel,
        out_shape=[jax.ShapeDtypeStruct(o, jnp.float32) for o in outs],
        in_specs=[pl.BlockSpec(memory_space=pltpu.VMEM)] * len(args),
        out_specs=[pl.BlockSpec(memory_space=pltpu.VMEM)] * len(outs),
        scratch_shapes=[pltpu.VMEM(o, jnp.float32) for o in scratch],
        compiler_params=pltpu.CompilerParams(vmem_limit_bytes=40 * 1024 * 1024),
        cost_estimate=pl.CostEstimate(flops=size * 20, bytes_accessed=size, transcendentals=0),
    )(*args)


def from_neighbours(first, last, axis):
    peers = lax.axis_size(axis)
    up = [(i, (i + 1) % peers) for i in range(peers - 1)]
    down = [(j, i) for i, j in up]
    return lax.ppermute(last, axis, up), lax.ppermute(first, axis, down)


def row_rims(fields):
    return from_neighbours(
        jnp.stack([f[:, :2] for f in fields]), jnp.stack([f[:, -2:] for f in fields]), "trow"
    )


def col_rims(fields):
    before, after = from_neighbours(
        jnp.stack([f[:, :, :2].swapaxes(1, 2) for f in fields]),
        jnp.stack([f[:, :, -2:].swapaxes(1, 2) for f in fields]),
        "tcol",
    )
    return jnp.concatenate([before, after], axis=2).swapaxes(2, 3)


def shards(
    theta,
    salt,
    velocity_x,
    velocity_y,
    land_mask,
    kappa,
    forcing,
    bottom,
    theta_cot,
    salt_cot,
    surface_cot,
):
    depth, rows, cols = theta.shape
    levels = lax.broadcasted_iota(jnp.int32, (depth, 1, 1), 0)
    wet = land_mask.astype(jnp.float32) * (levels < bottom[None]).astype(jnp.float32)
    rb, ra = row_rims([theta * wet, salt * wet, velocity_x, wet])
    rim = col_rims([theta * wet, salt * wet, velocity_y, wet])
    whole = (depth, rows, cols)
    theta_mix, salt_mix = call(
        forward_kernel,
        [whole, whole],
        [whole],
        (theta, salt, velocity_x, velocity_y, land_mask, kappa, forcing, bottom, rb, ra, rim),
    )
    zeta = conjugate(surface_cot, bottom, depth)
    theta_mu, salt_mu, kappa_grad, forcing_grad = call(
        mixing_kernel,
        [whole, whole, (depth - 1, rows, cols), (rows, cols)],
        [whole],
        (theta_cot, salt_cot, land_mask, kappa, bottom, zeta, theta_mix, salt_mix),
    )
    mu_rb, mu_ra = row_rims([theta_mu, salt_mu])
    mu_rim = col_rims([theta_mu, salt_mu])
    theta_grad, salt_grad = call(
        adjoint_kernel,
        [whole, whole],
        [],
        (theta_mu, salt_mu, velocity_x, velocity_y, land_mask, bottom, rb, ra, rim, mu_rb, mu_ra, mu_rim),
    )
    return (theta_grad, salt_grad, kappa_grad, forcing_grad)


def solution(mesh):
    in_specs = (
        P(None, "trow", "tcol"),
        P(None, "trow", "tcol"),
        P(None, "trow", "tcol"),
        P(None, "trow", "tcol"),
        P(None, "trow", "tcol"),
        P(None, "trow", "tcol"),
        P("trow", "tcol"),
        P("trow", "tcol"),
        P(None, "trow", "tcol"),
        P(None, "trow", "tcol"),
        P("trow", "tcol"),
    )
    out_specs = (
        P(None, "trow", "tcol"),
        P(None, "trow", "tcol"),
        P(None, "trow", "tcol"),
        P("trow", "tcol"),
    )
    return jax.shard_map(shards, mesh=mesh, in_specs=in_specs, out_specs=out_specs, check_vma=False)
```

```python
import functools
import jax
import jax.numpy as jnp
from jax import lax
from jax.experimental import pallas as pl
from jax.experimental.pallas import tpu as pltpu
from jax.sharding import PartitionSpec as P

ITERS = 4


def padded_2(array, sides, width):
    for axis, dim in sides:
        peers, length = (lax.axis_size(axis), array.shape[dim])
        up = [(i, (i + 1) % peers) for i in range(peers - 1)]
        down = [(j, i) for i, j in up]
        last = lax.slice_in_dim(array, length - width, length, axis=dim)
        leading = lax.slice_in_dim(array, 0, width, axis=dim)
        before = lax.ppermute(last, axis, up)
        after = lax.ppermute(leading, axis, down)
        array = jnp.concatenate([before, array, after], axis=dim)
    return array


def cut_along(array, start, count, axis_index):
    return lax.slice_in_dim(array, start, start + count, axis=axis_index)


def join(before, array, after, axis):
    return jnp.concatenate([before, array, after], axis=axis)


def open_faces(velocity, wet, first, count, axis):
    return (
        cut_along(velocity, first, count, axis)
        * cut_along(wet, first, count, axis)
        * cut_along(wet, first + 1, count, axis)
    )


def forward_change(tracer, opened, axis, length):
    centre = cut_along(tracer, 1, length + 1, axis) + cut_along(tracer, 2, length + 1, axis)
    outer = cut_along(tracer, 0, length + 1, axis) + cut_along(tracer, 3, length + 1, axis)
    fluxes = opened * (7.0 * centre - outer) * (1.0 / 12.0)
    return cut_along(fluxes, 1, length, axis) - cut_along(fluxes, 0, length, axis)


def adjoint_change(field, opened, axis, length):
    faces = opened * (cut_along(field, 0, length + 3, axis) - cut_along(field, 1, length + 3, axis))
    return (
        7.0 * (cut_along(faces, 2, length, axis) + cut_along(faces, 1, length, axis))
        - cut_along(faces, 3, length, axis)
        - cut_along(faces, 0, length, axis)
    ) * (1.0 / 12.0)


def wet_at(land, bottom, k):
    return jnp.where(k < bottom[...], land[k].astype(jnp.float32), 0.0)


def couple_at(kappa, land, bottom, k, depth):
    below = jnp.minimum(k + 1, depth - 1)
    value = kappa[jnp.minimum(k, depth - 2)] * wet_at(land, bottom, k) * wet_at(land, bottom, below)
    return jnp.where(k < depth - 1, value, 0.0)


def rows_of(rb, ra, index, k, own):
    return join(rb[index, k], own, ra[index, k], 0)


def cols_of(rim, index, k, own):
    edge = rim[index, k]
    return join(edge[:, :2], own, edge[:, 2:], 1)


def forward_kernel(
    theta, salt, vx, vy, land, kappa, forcing, bottom, rb, ra, rim, theta_mix, salt_mix, ratios
):
    depth, rows, cols = theta.shape

    def down(k, carry):
        couple_before, ratio_before, theta_before, salt_before = carry
        wet = wet_at(land, bottom, k)
        couple = couple_at(kappa, land, bottom, k, depth)
        inverse = 1.0 / (1.0 + couple_before - couple_before * ratio_before + couple)
        ratio = couple * inverse
        ratios[k] = ratio
        open_x = open_faces(
            rows_of(rb, ra, 2, k, vx[k]), rows_of(rb, ra, 3, k, wet), 1, rows + 1, 0
        )
        open_y = open_faces(cols_of(rim, 2, k, vy[k]), cols_of(rim, 3, k, wet), 1, cols + 1, 1)
        found = []
        for index, (tracer, before) in enumerate(((theta, theta_before), (salt, salt_before))):
            own = tracer[k]
            masked = own * wet
            adv = (
                own
                - forward_change(rows_of(rb, ra, index, k, masked), open_x, 0, rows)
                - forward_change(cols_of(rim, index, k, masked), open_y, 1, cols)
            )
            if index == 0:
                adv = adv + jnp.where(k == 0, forcing[...] * wet, 0.0)
            found.append((adv + couple_before * before) * inverse)
        theta_mix[k] = found[0]
        salt_mix[k] = found[1]
        return couple, ratio, found[0], found[1]

    zero = jnp.zeros((rows, cols), jnp.float32)
    _, _, theta_last, salt_last = lax.fori_loop(0, depth, down, (zero, zero, zero, zero))

    def up(i, carry):
        k = depth - 2 - i
        a = theta_mix[k] + ratios[k] * carry[0]
        b = salt_mix[k] + ratios[k] * carry[1]
        theta_mix[k] = a
        salt_mix[k] = b
        return a, b

    lax.fori_loop(0, depth - 1, up, (theta_last, salt_last))


def mixing_kernel(
    theta_cot, salt_cot, land, kappa, bottom, zeta, theta_mix, salt_mix,
    theta_mu, salt_mu, kappa_grad, forcing_grad, ratios
):
    depth, rows, cols = theta_cot.shape

    def down(k, carry):
        couple_before, ratio_before, theta_before, salt_before = carry
        lifted = wet_at(land, bottom, k) * zeta[...]
        couple = couple_at(kappa, land, bottom, k, depth)
        inverse = 1.0 / (1.0 + couple_before - couple_before * ratio_before + couple)
        ratio = couple * inverse
        ratios[k] = ratio
        a = (theta_cot[k] + 0.2 * lifted + couple_before * theta_before) * inverse
        b = (salt_cot[k] - 0.15 * lifted + couple_before * salt_before) * inverse
        theta_mu[k] = a
        salt_mu[k] = b
        return couple, ratio, a, b

    zero = jnp.zeros((rows, cols), jnp.float32)
    _, _, theta_last, salt_last = lax.fori_loop(0, depth, down, (zero, zero, zero, zero))

    def up(i, carry):
        k = depth - 2 - i
        a = theta_mu[k] + ratios[k] * carry[0]
        b = salt_mu[k] + ratios[k] * carry[1]
        theta_mu[k] = a
        salt_mu[k] = b
        opened = wet_at(land, bottom, k) * wet_at(land, bottom, k + 1)
        kappa_grad[k] = -opened * (
            (a - carry[0]) * (theta_mix[k] - theta_mix[k + 1])
            + (b - carry[1]) * (salt_mix[k] - salt_mix[k + 1])
        )
        return a, b

    theta_top, _ = lax.fori_loop(0, depth - 1, up, (theta_last, salt_last))
    forcing_grad[...] = zeta[...] + wet_at(land, bottom, 0) * theta_top


def adjoint_kernel(
    theta_mu, salt_mu, vx, vy, land, bottom, rb, ra, rim, mu_rb, mu_ra, mu_rim, theta_grad, salt_grad
):
    depth, rows, cols = theta_mu.shape

    def level(k, carry):
        wet = wet_at(land, bottom, k)
        open_x = open_faces(
            rows_of(rb, ra, 2, k, vx[k]), rows_of(rb, ra, 3, k, wet), 0, rows + 3, 0
        )
        open_y = open_faces(cols_of(rim, 2, k, vy[k]), cols_of(rim, 3, k, wet), 0, cols + 3, 1)
        for index, (field, out) in enumerate(((theta_mu, theta_grad), (salt_mu, salt_grad))):
            own = field[k]
            out[k] = own - wet * (
                adjoint_change(rows_of(mu_rb, mu_ra, index, k, own), open_x, 0, rows)
                + adjoint_change(cols_of(mu_rim, index, k, own), open_y, 1, cols)
            )
        return carry

    lax.fori_loop(0, depth, level, 0)


LOW, HIGH = 0.2, 9.2
CENTRE, RADIUS = (HIGH + LOW) / 2, (HIGH - LOW) / 2


def times_operator(poly):
    out = [0.0] * (len(poly) + 1)
    for k, c in enumerate(poly):
        out[k] = out[k] + CENTRE * c
        if k == 0:
            out[1] = out[1] + RADIUS * c
        else:
            out[k + 1] = out[k + 1] + 0.5 * RADIUS * c
            out[k - 1] = out[k - 1] + 0.5 * RADIUS * c
    return out


def inner(p, q, moments):
    total = 0.0
    for i, a in enumerate(p):
        for j, b in enumerate(q):
            total = total + a * b * (0.5 * (moments[i + j] + moments[abs(i - j)]))
    return total


def add_scaled(p, scale, q):
    size = max(len(p), len(q))
    p = p + [0.0] * (size - len(p))
    q = q + [0.0] * (size - len(q))
    return [a + scale * b for a, b in zip(p, q)]


def weights_from(moments):
    residual = [jnp.ones_like(moments[0])]
    direction = residual
    result = []
    norm_now = moments[0]
    for iteration in range(ITERS):
        image = times_operator(direction)
        step = norm_now / inner(direction, image, moments)
        result = add_scaled(result, step, direction)
        if iteration + 1 < ITERS:
            residual = add_scaled(residual, -step, image)
            norm_next = inner(residual, residual, moments)
            direction = add_scaled(residual, norm_next / norm_now, direction)
            norm_now = norm_next
    return result


MESH = pl.DeviceIdType.MESH


def gather_kernel(lanes, piece, out, line, plane, own_sem, send, recv):
    rows, cols = lax.axis_size("trow"), lax.axis_size("tcol")
    row, col = lax.axis_index("trow"), lax.axis_index("tcol")
    peers = [(row, lax.rem(col + d, cols)) for d in range(1, cols)]
    peers += [(lax.rem(row + d, rows), col) for d in range(1, rows)]
    barrier = pltpu.get_barrier_semaphore()
    for peer in peers:
        pl.semaphore_signal(barrier, inc=1, device_id=peer, device_id_type=MESH)
    keep = pltpu.make_async_copy(piece, line.at[0], own_sem.at[0])
    keep.start()
    keep.wait()
    pl.semaphore_wait(barrier, len(peers))

    def remote(src, dst, index):
        return pltpu.make_async_remote_copy(
            src_ref=src,
            dst_ref=dst,
            send_sem=send.at[index],
            recv_sem=recv.at[index],
            device_id=peers[index],
            device_id_type=MESH,
        )

    along = [remote(piece, line.at[d], d - 1) for d in range(1, cols)]
    for copy in along:
        copy.start()
    for copy in along:
        copy.wait()
    across = [remote(line, plane.at[d - 1], cols + d - 2) for d in range(1, rows)]
    for copy in across:
        copy.start()
    total = line[0]
    for d in range(1, cols):
        total = total + line[d]
    for copy in across:
        copy.wait()
    for d in range(rows - 1):
        for e in range(cols):
            total = total + plane[d, e]
    out[...] = total


def sum_everywhere(sums):
    rows, cols = lax.axis_size("trow"), lax.axis_size("tcol")
    lanes = 128
    piece = jnp.broadcast_to(jnp.pad(sums, (0, lanes - sums.shape[0]))[None], (8, lanes))
    count = rows + cols - 2
    total = pl.pallas_call(
        functools.partial(gather_kernel, lanes),
        out_shape=jax.ShapeDtypeStruct((8, lanes), jnp.float32),
        in_specs=[pl.BlockSpec(memory_space=pltpu.VMEM)],
        out_specs=pl.BlockSpec(memory_space=pltpu.VMEM),
        scratch_shapes=[
            pltpu.VMEM((cols, 8, lanes), jnp.float32),
            pltpu.VMEM((rows - 1, cols, 8, lanes), jnp.float32),
            pltpu.SemaphoreType.DMA((1,)),
            pltpu.SemaphoreType.DMA((count,)),
            pltpu.SemaphoreType.DMA((count,)),
        ],
        compiler_params=pltpu.CompilerParams(collective_id=0, has_side_effects=True),
    )(piece)
    return total[0, : sums.shape[0]]


def conjugate(target, bottom, depth):
    rows, cols = target.shape
    rim = ITERS
    padded = padded_2(jnp.stack([target, bottom.astype(jnp.float32)]), (("trow", 1), ("tcol", 2)), rim)
    row = lax.broadcasted_iota(jnp.int32, (rows + 2 * rim, 1), 0) - rim + lax.axis_index("trow") * rows
    col = lax.broadcasted_iota(jnp.int32, (1, cols + 2 * rim), 1) - rim + lax.axis_index("tcol") * cols
    inside = ((row >= 0) & (row < rows * lax.axis_size("trow"))) & (
        (col >= 0) & (col < cols * lax.axis_size("tcol"))
    )
    scaled = (4.2 - CENTRE + padded[1] / depth) / RADIUS
    basis = [padded[0]]
    for k in range(ITERS):
        field = basis[-1]
        edge = k + 1
        beside = field[2:, 1:-1] + field[:-2, 1:-1] + field[1:-1, 2:] + field[1:-1, :-2]
        image = scaled[edge:-edge, edge:-edge] * field[1:-1, 1:-1] - beside * (1.0 / RADIUS)
        if k > 0:
            image = 2.0 * image - basis[-2][2:-2, 2:-2]
        basis.append(jnp.where(inside[edge:-edge, edge:-edge], image, 0.0))
    own = [f[rim - k : rim - k + rows, rim - k : rim - k + cols] for k, f in enumerate(basis)]
    sums = [jnp.sum(own[0] * own[k]) for k in range(5)]
    sums += [jnp.sum(own[2] * own[3]), jnp.sum(own[3] * own[3]), jnp.sum(own[3] * own[4])]
    m = list(sum_everywhere(jnp.stack(sums)))
    m = m[:5] + [2.0 * m[5] - m[1], 2.0 * m[6] - m[0], 2.0 * m[7] - m[1]]
    weights = weights_from(m)
    result = weights[0] * own[0]
    for k in range(1, ITERS):
        result = result + weights[k] * own[k]
    return result


def call(kernel, outs, scratch, args):
    size = sum(a.size for a in args) * 4
    return pl.pallas_call(
        kernel,
        out_shape=[jax.ShapeDtypeStruct(o, jnp.float32) for o in outs],
        in_specs=[pl.BlockSpec(memory_space=pltpu.VMEM)] * len(args),
        out_specs=[pl.BlockSpec(memory_space=pltpu.VMEM)] * len(outs),
        scratch_shapes=[pltpu.VMEM(o, jnp.float32) for o in scratch],
        compiler_params=pltpu.CompilerParams(vmem_limit_bytes=40 * 1024 * 1024),
        cost_estimate=pl.CostEstimate(flops=size * 20, bytes_accessed=size, transcendentals=0),
    )(*args)


def from_neighbours(first, last, axis):
    peers = lax.axis_size(axis)
    up = [(i, (i + 1) % peers) for i in range(peers - 1)]
    down = [(j, i) for i, j in up]
    return lax.ppermute(last, axis, up), lax.ppermute(first, axis, down)


def row_rims(fields):
    return from_neighbours(
        jnp.stack([f[:, :2] for f in fields]), jnp.stack([f[:, -2:] for f in fields]), "trow"
    )


def col_rims(fields):
    before, after = from_neighbours(
        jnp.stack([f[:, :, :2].swapaxes(1, 2) for f in fields]),
        jnp.stack([f[:, :, -2:].swapaxes(1, 2) for f in fields]),
        "tcol",
    )
    return jnp.concatenate([before, after], axis=2).swapaxes(2, 3)


def shards(
    theta,
    salt,
    velocity_x,
    velocity_y,
    land_mask,
    kappa,
    forcing,
    bottom,
    theta_cot,
    salt_cot,
    surface_cot,
):
    depth, rows, cols = theta.shape
    levels = lax.broadcasted_iota(jnp.int32, (depth, 1, 1), 0)
    wet = land_mask.astype(jnp.float32) * (levels < bottom[None]).astype(jnp.float32)
    rb, ra = row_rims([theta * wet, salt * wet, velocity_x, wet])
    rim = col_rims([theta * wet, salt * wet, velocity_y, wet])
    whole = (depth, rows, cols)
    theta_mix, salt_mix = call(
        forward_kernel,
        [whole, whole],
        [whole],
        (theta, salt, velocity_x, velocity_y, land_mask, kappa, forcing, bottom, rb, ra, rim),
    )
    zeta = conjugate(surface_cot, bottom, depth)
    theta_mu, salt_mu, kappa_grad, forcing_grad = call(
        mixing_kernel,
        [whole, whole, (depth - 1, rows, cols), (rows, cols)],
        [whole],
        (theta_cot, salt_cot, land_mask, kappa, bottom, zeta, theta_mix, salt_mix),
    )
    mu_rb, mu_ra = row_rims([theta_mu, salt_mu])
    mu_rim = col_rims([theta_mu, salt_mu])
    theta_grad, salt_grad = call(
        adjoint_kernel,
        [whole, whole],
        [],
        (theta_mu, salt_mu, velocity_x, velocity_y, land_mask, bottom, rb, ra, rim, mu_rb, mu_ra, mu_rim),
    )
    return (theta_grad, salt_grad, kappa_grad, forcing_grad)


def solution(mesh):
    in_specs = (
        P(None, "trow", "tcol"),
        P(None, "trow", "tcol"),
        P(None, "trow", "tcol"),
        P(None, "trow", "tcol"),
        P(None, "trow", "tcol"),
        P(None, "trow", "tcol"),
        P("trow", "tcol"),
        P("trow", "tcol"),
        P(None, "trow", "tcol"),
        P(None, "trow", "tcol"),
        P("trow", "tcol"),
    )
    out_specs = (
        P(None, "trow", "tcol"),
        P(None, "trow", "tcol"),
        P(None, "trow", "tcol"),
        P("trow", "tcol"),
    )
    return jax.shard_map(shards, mesh=mesh, in_specs=in_specs, out_specs=out_specs, check_vma=False)
```
